32 devices in a mesh: rep: 2 (over x), fsdp: 16 (over z, y, core).
Axes of the slice: x: 2, y: 2, z: 4, core: 2. Of those that a mesh axis runs over, the one named last changes fastest.
Arguments:
- residual_input: bfloat16 [7168, 2048], P(('rep', 'fsdp')), may hold values from -6 to 6
- document_index: int32 [32, 224], P(('rep', 'fsdp')), may hold values from 0 to 55, never falling along the last dimension, each value on 1 to 112 neighbouring positions
- adapter_index: int32 [32], P(('rep', 'fsdp')), may hold values from 0 to 7
- attention_gain: bfloat16 [1, 2048], replicated, may hold values from 0.099609375 to 1.8984375
- feedforward_gain: bfloat16 [1, 2048], replicated, may hold values from 0.099609375 to 1.8984375
- query_weight: bfloat16 [1, 2048, 2048], P(None, 'fsdp'), may hold values from -0.5 to 0.5
- key_weight: bfloat16 [1, 2048, 512], P(None, 'fsdp'), may hold values from -0.5 to 0.5
- value_weight: bfloat16 [1, 2048, 512], P(None, 'fsdp'), may hold values from -0.125 to 0.125
- output_weight: bfloat16 [1, 2048, 2048], P(None, 'fsdp'), may hold values from -1 to 1
- gate_weight: bfloat16 [1, 2048, 8192], P(None, None, 'fsdp'), may hold values from -0.125 to 0.125
- up_weight: bfloat16 [1, 2048, 8192], P(None, None, 'fsdp'), may hold values from -0.125 to 0.125
- down_weight: bfloat16 [1, 8192, 2048], P(None, 'fsdp'), may hold values from -0.75 to 0.75
- attention_input_factor: bfloat16 [1, 8, 2048, 48], P(None, None, 'fsdp'), may hold values from -0.125 to 0.125
- output_input_factor: bfloat16 [1, 8, 2048, 16], P(None, None, 'fsdp'), may hold values from -0.125 to 0.125
- feedforward_input_factor: bfloat16 [1, 8, 2048, 32], P(None, None, 'fsdp'), may hold values from -0.125 to 0.125
- down_input_factor: bfloat16 [1, 8, 8192, 16], P(None, None, 'fsdp'), may hold values from -0.0625 to 0.0625
- query_output_factor: bfloat16 [1, 8, 16, 2048], P(None, None, None, 'fsdp'), may hold values from -3 to 3
- key_output_factor: bfloat16 [1, 8, 16, 512], P(None, None, None, 'fsdp'), may hold values from -3 to 3
- value_output_factor: bfloat16 [1, 8, 16, 512], P(None, None, None, 'fsdp'), may hold values from -0.75 to 0.75
- output_output_factor: bfloat16 [1, 8, 16, 2048], P(None, None, None, 'fsdp'), may hold values from -4 to 4
- gate_output_factor: bfloat16 [1, 8, 16, 8192], P(None, None, None, 'fsdp'), may hold values from -0.75 to 0.75
- up_output_factor: bfloat16 [1, 8, 16, 8192], P(None, None, None, 'fsdp'), may hold values from -0.75 to 0.75
- down_output_factor: bfloat16 [1, 8, 16, 2048], P(None, None, None, 'fsdp'), may hold values from -6 to 6
- cotangent: bfloat16 [7168, 2048], P(('rep', 'fsdp')), may hold values from -6 to 6
Outputs:
- hidden_out: bfloat16 [7168, 2048], P(('rep', 'fsdp'))
- input_grad: float32 [7168, 2048], P(('rep', 'fsdp'))
- grad_lora_a_attn: float32 [1, 8, 2048, 48], P(None, None, 'fsdp')
- grad_lora_a_out: float32 [1, 8, 2048, 16], P(None, None, 'fsdp')
- grad_lora_a_mlp: float32 [1, 8, 2048, 32], P(None, None, 'fsdp')
- grad_lora_a_down: float32 [1, 8, 8192, 16], P(None, None, 'fsdp')
- grad_lora_b_query: float32 [1, 8, 16, 2048], P(None, None, None, 'fsdp')
- grad_lora_b_key: float32 [1, 8, 16, 512], P(None, None, None, 'fsdp')
- grad_lora_b_value: float32 [1, 8, 16, 512], P(None, None, None, 'fsdp')
- grad_lora_b_out: float32 [1, 8, 16, 2048], P(None, None, None, 'fsdp')
- grad_lora_b_gate: float32 [1, 8, 16, 8192], P(None, None, None, 'fsdp')
- grad_lora_b_up: float32 [1, 8, 16, 8192], P(None, None, None, 'fsdp')
- grad_lora_b_down: float32 [1, 8, 16, 2048], P(None, None, None, 'fsdp')
The draws below stay inside these ranges and needn't reach their ends.
Inputs may be any that keep to these rules, and one draw needn't show every extreme that they name: `document_index`: within a sequence the ids never fall, so each document is one run of equal ids of at most 112 tokens; some document has exactly that many. `adapter_index`: the adapter that all tokens of the sequence use.
All inputs are finite; a program needn't handle non-finite values.
Results may differ from the reference program's by a relative error of at most 0.02.
The reference program's roundings to bfloat16 on the way count: a program that leaves them out, or rounds other values in their place, can miss the bound.
Values may be sent and summed in bfloat16 or wider, within the bound.
No kernel may reach another device: no remote copies, remote signals or barrier semaphores. Data moves between devices by JAX's collectives and lax.ppermute only.
A program may use at most 320 MiB of HBM per device.

```python
import math
import jax
import jax.numpy as jnp
import numpy as np
from jax import lax

MODEL_WIDTH = 2048
HEADS = 32
KV_HEADS = 8
HEAD_DIM = 64
HIDDEN_UNITS = 8192
ADAPTER_RANK = 16
ADAPTER_COUNT = 8
LAYER_COUNT = 1
TOK_DEV = 224
QUERY_WIDTH = 2048
KEY_VALUE_WIDTH = 512
SEQS = 32
TOKENS = 7168


def place_ends(result, stream_key, least, high):
    extent = result.shape
    index_at = [jax.random.randint(jax.random.fold_in(stream_key, axis), (), 0, extent[axis]) for axis in range(len(extent))]
    result = result.at[tuple(index_at)].set(least)
    longest = extent.index(max(extent))
    index_at[longest] = (index_at[longest] + 1) % extent[longest]
    return result.at[tuple(index_at)].set(high)


def block_scale(key, dims, pieces, smallest, top_value):
    def one(dim, blocks):
        heights = jax.random.uniform(jax.random.fold_in(jax.random.fold_in(key, 6), dim), (blocks,), jnp.float32, smallest / len(pieces), top_value / len(pieces))
        return jnp.repeat(jnp.exp(heights), dims[dim] // blocks).reshape((-1,) + (1,) * (len(dims) - dim - 1))

    gain = one(*pieces[0])
    for cut in pieces[1:]:
        gain = gain * one(*cut)
    return gain


def length_profile(count, total, bound, skew):
    portions = [(1 << 20) // math.isqrt(rank ** skew) + 1 for rank in range(2, count + 1)]
    surplus, given = total - bound - (count - 1), [1] * (count - 1)
    while surplus > 0:
        candidates = [i for i in range(count - 1) if given[i] < bound]
        whole, left = sum([portions[i] for i in candidates]), surplus
        for i in candidates:
            extra = min(bound - given[i], max(1, left * portions[i] // whole), surplus)
            given[i] = given[i] + extra
            surplus = surplus - extra
    return np.array([bound] + given)


def ragged_sizes(stream_key, count, total, bound, slope):
    if count == 2:
        one = jax.random.randint(stream_key, (), max(1, total - bound), min(bound, total - 1) + 1)
        return jnp.stack([one, total - one])
    lengths = jnp.asarray(length_profile(count, total, bound, slope), jnp.int32)
    twos = (count - 1) // 2
    source_of, sink = lengths[1:1 + 2 * twos:2], lengths[2:2 + 2 * twos:2]
    slack = jnp.minimum(source_of - 1, bound - sink)
    moved = jax.random.randint(jax.random.fold_in(stream_key, 1), (twos,), 0, 1 << 20) % (slack + 1)
    lengths = lengths.at[1:1 + 2 * twos:2].set(source_of - moved).at[2:2 + 2 * twos:2].set(sink + moved)
    return lengths[jax.random.permutation(jax.random.fold_in(stream_key, 2), count)]


def normal_values(rng, extent, width, limit, cuts=(), held_as=jnp.bfloat16):
    factor_of = block_scale(rng, extent, cuts, -0.22, 0.18) if cuts else 1.0
    values = jax.random.normal(rng, extent, jnp.float32) * width * factor_of
    return jnp.minimum(jnp.maximum(values, -limit), limit).astype(held_as)


def setup_inputs(seed: int = 0) -> dict:
    key_list = jax.random.split(jax.random.key(seed), 25)
    residual_input = normal_values(key_list[0], (TOKENS, MODEL_WIDTH), 1.0, 6.0, ((0, 32),))
    document_index = jax.vmap(lambda own: jnp.searchsorted(jnp.cumsum(ragged_sizes(own, TOK_DEV // 4, TOK_DEV, TOK_DEV // 2, 2)), jnp.arange(TOK_DEV), side="right"))(jax.random.split(key_list[1], SEQS)).reshape((SEQS, TOK_DEV)).astype(jnp.int32)
    adapter_index = place_ends(jax.random.randint(key_list[2], (SEQS,), 0, ADAPTER_COUNT), jax.random.fold_in(key_list[2], 1), 0, ADAPTER_COUNT - 1).astype(jnp.int32)
    attention_gain = jnp.clip(1.0 + 0.18 * jax.random.normal(key_list[3], (LAYER_COUNT, MODEL_WIDTH), jnp.float32), 0.099609375, 1.8984375).astype(jnp.bfloat16)
    feedforward_gain = jnp.clip(1.0 + 0.18 * jax.random.normal(key_list[4], (LAYER_COUNT, MODEL_WIDTH), jnp.float32), 0.099609375, 1.8984375).astype(jnp.bfloat16)
    query_weight = normal_values(key_list[5], (LAYER_COUNT, MODEL_WIDTH, QUERY_WIDTH), (MODEL_WIDTH // 16) ** -0.5, 0.5, ((1, 16),))
    key_weight = normal_values(key_list[6], (LAYER_COUNT, MODEL_WIDTH, KEY_VALUE_WIDTH), (MODEL_WIDTH // 16) ** -0.5, 0.5, ((1, 16),))
    value_weight = normal_values(key_list[7], (LAYER_COUNT, MODEL_WIDTH, KEY_VALUE_WIDTH), MODEL_WIDTH ** -0.5, 0.125, ((1, 16),))
    output_weight = normal_values(key_list[8], (LAYER_COUNT, QUERY_WIDTH, MODEL_WIDTH), (max(QUERY_WIDTH // 64, 1)) ** -0.5, 1.0, ((1, 16),))
    gate_weight = normal_values(key_list[9], (LAYER_COUNT, MODEL_WIDTH, HIDDEN_UNITS), MODEL_WIDTH ** -0.5, 0.125, ((2, 16),))
    up_weight = normal_values(key_list[10], (LAYER_COUNT, MODEL_WIDTH, HIDDEN_UNITS), MODEL_WIDTH ** -0.5, 0.125, ((2, 16),))
    down_weight = normal_values(key_list[11], (LAYER_COUNT, HIDDEN_UNITS, MODEL_WIDTH), (max(HIDDEN_UNITS // 128, 1)) ** -0.5, 0.75, ((1, 16),))
    attention_input_factor = normal_values(key_list[12], (LAYER_COUNT, ADAPTER_COUNT, MODEL_WIDTH, 3 * ADAPTER_RANK), MODEL_WIDTH ** -0.5, 0.125, ((2, 16),))
    output_input_factor = normal_values(key_list[13], (LAYER_COUNT, ADAPTER_COUNT, QUERY_WIDTH, ADAPTER_RANK), QUERY_WIDTH ** -0.5, 0.125, ((2, 16),))
    feedforward_input_factor = normal_values(key_list[14], (LAYER_COUNT, ADAPTER_COUNT, MODEL_WIDTH, 2 * ADAPTER_RANK), MODEL_WIDTH ** -0.5, 0.125, ((2, 16),))
    down_input_factor = normal_values(key_list[15], (LAYER_COUNT, ADAPTER_COUNT, HIDDEN_UNITS, ADAPTER_RANK), HIDDEN_UNITS ** -0.5, 0.0625, ((2, 16),))
    query_output_factor = normal_values(key_list[16], (LAYER_COUNT, ADAPTER_COUNT, ADAPTER_RANK, QUERY_WIDTH), (max(ADAPTER_RANK // 4, 1)) ** -0.5, 3.0, ((3, 16),))
    key_output_factor = normal_values(key_list[17], (LAYER_COUNT, ADAPTER_COUNT, ADAPTER_RANK, KEY_VALUE_WIDTH), (max(ADAPTER_RANK // 4, 1)) ** -0.5, 3.0, ((3, 16),))
    value_output_factor = normal_values(key_list[18], (LAYER_COUNT, ADAPTER_COUNT, ADAPTER_RANK, KEY_VALUE_WIDTH), (4 * ADAPTER_RANK) ** -0.5, 0.75, ((3, 16),))
    output_output_factor = normal_values(key_list[19], (LAYER_COUNT, ADAPTER_COUNT, ADAPTER_RANK, MODEL_WIDTH), (max(ADAPTER_RANK // 8, 1)) ** -0.5, 4.0, ((3, 16),))
    gate_output_factor = normal_values(key_list[20], (LAYER_COUNT, ADAPTER_COUNT, ADAPTER_RANK, HIDDEN_UNITS), (4 * ADAPTER_RANK) ** -0.5, 0.75, ((3, 16),))
    up_output_factor = normal_values(key_list[21], (LAYER_COUNT, ADAPTER_COUNT, ADAPTER_RANK, HIDDEN_UNITS), (4 * ADAPTER_RANK) ** -0.5, 0.75, ((3, 16),))
    down_output_factor = normal_values(key_list[22], (LAYER_COUNT, ADAPTER_COUNT, ADAPTER_RANK, MODEL_WIDTH), (max(ADAPTER_RANK // 16, 1)) ** -0.5, 6.0, ((3, 16),))
    cotangent = normal_values(key_list[23], (TOKENS, MODEL_WIDTH), 1.0, 6.0, ((0, 32),))
    return dict(residual_input=residual_input, document_index=document_index, adapter_index=adapter_index, attention_gain=attention_gain, feedforward_gain=feedforward_gain, query_weight=query_weight, key_weight=key_weight, value_weight=value_weight, output_weight=output_weight, gate_weight=gate_weight, up_weight=up_weight, down_weight=down_weight, attention_input_factor=attention_input_factor, output_input_factor=output_input_factor, feedforward_input_factor=feedforward_input_factor, down_input_factor=down_input_factor, query_output_factor=query_output_factor, key_output_factor=key_output_factor, value_output_factor=value_output_factor, output_output_factor=output_output_factor, gate_output_factor=gate_output_factor, up_output_factor=up_output_factor, down_output_factor=down_output_factor, cotangent=cotangent)


@jax.custom_vjp
def low(v):
    return lax.optimization_barrier(v.astype(jnp.bfloat16)).astype(jnp.float32)

@jax.custom_vjp
def low_back(v):
    return v

def low_keep(v):
    return (low(v), None)

def low_pass(kept, grad):
    return (grad,)

def back_keep(v):
    return (v, None)

def back_low(kept, grad):
    return (low(grad),)
low.defvjp(low_keep, low_pass)
low_back.defvjp(back_keep, back_low)
eps = 1e-05
attn_mult = 0.015625
resid_mult = 0.22
rope_base = 10000000.0
neg_big = -1e+30
highest = lax.Precision.HIGHEST

def batch_dot(form, left_op, right_op):
    return jnp.einsum(form, left_op, right_op, precision=highest)

def rms_scale(stream, gain_row):
    return stream * lax.rsqrt(lax.optimization_barrier(jnp.mean(stream * stream, axis=-1, keepdims=True)) + eps) * gain_row

def rope_tables(seq_len, head_dim):
    half_dim = head_dim // 2
    frequency = rope_base ** (-2.0 * jnp.arange(half_dim, dtype=jnp.float32) / head_dim)
    angles = jnp.arange(seq_len, dtype=jnp.float32)[:, None] * frequency[None, :]
    return (jnp.cos(angles)[:, None, :], jnp.sin(angles)[:, None, :])

def rotate(vector, cosine, sine_table):
    half_dim = vector.shape[-1] // 2
    former = vector[..., :half_dim]
    latter = vector[..., half_dim:]
    return jnp.concatenate([former * cosine - latter * sine_table, latter * cosine + former * sine_table], axis=-1)

def one_layer(stream, allowed, cosine, sine_table, frozen, adapt):
    attn_gain_row, mlp_gain_row, query_w, key_w, value_w, out_w, gate_w, up_w, down_w = frozen
    down_attn, down_out, down_mlp, down_inner, lift_query, lift_key, lift_value, lift_out, lift_gate, lift_up, lift_down = adapt
    groups = stream.shape[0]
    seq_len = stream.shape[1]
    normed = low(rms_scale(stream, attn_gain_row))
    small_attn = low_back(low(batch_dot('gsd,gdr->gsr', normed, down_attn)))
    query_raw = low_back(batch_dot('gsd,de->gse', normed, query_w) + batch_dot('gsr,gre->gse', small_attn[..., :ADAPTER_RANK], lift_query))
    key_raw = low_back(batch_dot('gsd,de->gse', normed, key_w) + batch_dot('gsr,gre->gse', small_attn[..., ADAPTER_RANK:2 * ADAPTER_RANK], lift_key))
    value_raw = low_back(batch_dot('gsd,de->gse', normed, value_w) + batch_dot('gsr,gre->gse', small_attn[..., 2 * ADAPTER_RANK:], lift_value))
    queries = low(rotate(query_raw.reshape(groups, seq_len, HEADS, HEAD_DIM), cosine, sine_table))
    key_rot = low(rotate(key_raw.reshape(groups, seq_len, KV_HEADS, HEAD_DIM), cosine, sine_table))
    values = low(value_raw.reshape(groups, seq_len, KV_HEADS, HEAD_DIM))
    grouped = queries.reshape(groups, seq_len, KV_HEADS, HEADS // KV_HEADS, HEAD_DIM)
    scores = low_back(batch_dot('gskhe,gtke->gkhst', grouped, key_rot) * attn_mult)
    scores = jnp.where(allowed[:, None, None], scores, neg_big)
    row_top = lax.optimization_barrier(jnp.max(scores, axis=-1, keepdims=True))
    exp_scores = jnp.exp(scores - row_top)
    probs = low(exp_scores / lax.optimization_barrier(jnp.sum(exp_scores, axis=-1, keepdims=True)))
    mixed = batch_dot('gkhst,gtke->gskhe', probs, values).reshape(groups, seq_len, HEADS * HEAD_DIM)
    mixed = low(low_back(mixed))
    small_out = low_back(low(batch_dot('gsq,gqr->gsr', mixed, down_out)))
    branch = low_back(batch_dot('gsq,qd->gsd', mixed, out_w) + batch_dot('gsr,grd->gsd', small_out, lift_out))
    after_attn = stream + resid_mult * branch
    normed_mlp = low(rms_scale(after_attn, mlp_gain_row))
    small_mlp = low_back(low(batch_dot('gsd,gdr->gsr', normed_mlp, down_mlp)))
    gate_act = low_back(batch_dot('gsd,df->gsf', normed_mlp, gate_w) + batch_dot('gsr,grf->gsf', small_mlp[..., :ADAPTER_RANK], lift_gate))
    up_proj = low_back(batch_dot('gsd,df->gsf', normed_mlp, up_w) + batch_dot('gsr,grf->gsf', small_mlp[..., ADAPTER_RANK:], lift_up))
    active = low(gate_act * jax.nn.sigmoid(gate_act) * up_proj)
    small_down = low_back(low(batch_dot('gsf,gfr->gsr', active, down_inner)))
    branch_mlp = low_back(batch_dot('gsf,fd->gsd', active, down_w) + batch_dot('gsr,grd->gsd', small_down, lift_down))
    return after_attn + resid_mult * branch_mlp

def reference(residual_input, document_index, adapter_index, attention_gain, feedforward_gain, query_weight, key_weight, value_weight, output_weight, gate_weight, up_weight, down_weight, attention_input_factor, output_input_factor, feedforward_input_factor, down_input_factor, query_output_factor, key_output_factor, value_output_factor, output_output_factor, gate_output_factor, up_output_factor, down_output_factor, cotangent):
    frozen = tuple((member_entry.astype(jnp.float32) for member_entry in (attention_gain, feedforward_gain, query_weight, key_weight, value_weight, output_weight, gate_weight, up_weight, down_weight)))
    adapter_bundle = tuple((member_entry.astype(jnp.float32) for member_entry in (attention_input_factor, output_input_factor, feedforward_input_factor, down_input_factor, query_output_factor, key_output_factor, value_output_factor, output_output_factor, gate_output_factor, up_output_factor, down_output_factor)))
    group = 1
    while group * 2 * TOK_DEV <= 4096 and SEQS % (group * 2) == 0:
        group = group * 2
    blocks = SEQS // group
    inputs = residual_input.astype(jnp.float32).reshape(blocks, group, TOK_DEV, MODEL_WIDTH)
    grads_in = cotangent.astype(jnp.float32).reshape(blocks, group, TOK_DEV, MODEL_WIDTH)
    segments = document_index.reshape(blocks, group, TOK_DEV)
    chosen = adapter_index.reshape(blocks, group)
    cosine, sine_table = rope_tables(TOK_DEV, HEAD_DIM)
    positions = jnp.arange(TOK_DEV, dtype=jnp.int32)
    causal = positions[None, :] <= positions[:, None]

    def forward(stream, allowed, picked, adapt):
        for layer_index in range(LAYER_COUNT):
            layer_frozen = tuple((member_entry[layer_index] for member_entry in frozen))
            layer_adapt = tuple((member_entry[layer_index][picked] for member_entry in adapt))
            stream = one_layer(stream, allowed, cosine, sine_table, layer_frozen, layer_adapt)
        return stream

    def block_step(totals, block):
        stream, grad_out, segment_block, picked = block
        allowed = (segment_block[:, :, None] == segment_block[:, None, :]) & causal[None]
        output, pullback = jax.vjp(lambda start, adapt: forward(start, allowed, picked, adapt), stream, adapter_bundle)
        grad_stream, grad_adapt = pullback(grad_out)
        totals = tuple((total_sum + piece for total_sum, piece in zip(totals, grad_adapt)))
        return (totals, (output, grad_stream))
    zeros = tuple((jnp.zeros(member_entry.shape, jnp.float32) for member_entry in adapter_bundle))
    totals, (outputs, grads) = lax.scan(block_step, zeros, (inputs, grads_in, segments, chosen))
    hidden_out = outputs.reshape(TOKENS, MODEL_WIDTH).astype(jnp.bfloat16)
    input_grad = grads.reshape(TOKENS, MODEL_WIDTH)
    return (hidden_out, input_grad, totals[0], totals[1], totals[2], totals[3], totals[4], totals[5], totals[6], totals[7], totals[8], totals[9], totals[10])
```

```python
from functools import partial

import jax
import jax.numpy as jnp
from jax import lax
from jax.sharding import PartitionSpec as P

HEADS = 32
KV_HEADS = 8
HEAD_DIM = 64
ADAPTER_RANK = 16
ADAPTER_COUNT = 8


eps = 1e-05
attn_mult = 0.015625
resid_mult = 0.22
rope_base = 10000000.0
neg_big = -1e30


def plain_dot(left_op, right_op):
    return jnp.dot(left_op, right_op, preferred_element_type=jnp.float32)


def inner_dot(left_op, right_op):
    return lax.dot_general(
        left_op, right_op, (((0,), (0,)), ((), ())), preferred_element_type=jnp.float32
    )


def outer_dot(left_op, right_op):
    return lax.dot_general(
        left_op, right_op, (((1,), (1,)), ((), ())), preferred_element_type=jnp.float32
    )


def norm_forward(stream, gain_row):
    inv_scale = lax.rsqrt(jnp.mean(stream * stream, axis=-1, keepdims=True) + eps)
    return ((stream * inv_scale * gain_row).astype(jnp.bfloat16), inv_scale)


def norm_backward(grad_normed, stream, inv_scale, gain_row):
    weighted = grad_normed * gain_row
    return inv_scale * weighted - stream * inv_scale**3 * jnp.mean(
        weighted * stream, axis=-1, keepdims=True
    )


def rope_tables(seq_len, head_dim):
    half_dim = head_dim // 2
    frequency = rope_base ** (-2.0 * jnp.arange(half_dim, dtype=jnp.float32) / head_dim)
    angles = jnp.arange(seq_len, dtype=jnp.float32)[:, None] * frequency[None, :]
    return (jnp.cos(angles)[:, None, :], jnp.sin(angles)[:, None, :])


def rotate(vector, cosine, sine_table):
    half_dim = vector.shape[-1] // 2
    former = vector[..., :half_dim]
    latter = vector[..., half_dim:]
    return jnp.concatenate(
        [former * cosine - latter * sine_table, latter * cosine + former * sine_table], axis=-1
    )


def rotate_back(vector, cosine, sine_table):
    half_dim = vector.shape[-1] // 2
    former = vector[..., :half_dim]
    latter = vector[..., half_dim:]
    return jnp.concatenate(
        [former * cosine + latter * sine_table, latter * cosine - former * sine_table], axis=-1
    )


def masked_scores(grouped, key_rot, allowed):
    scores = (
        jnp.einsum("skhe,tke->khst", grouped, key_rot, preferred_element_type=jnp.float32)
        * attn_mult
    )
    return jnp.where(allowed, scores, neg_big)


def gate_grads(grad_active, gate_act, up_proj):
    sigmoid_gate = jax.nn.sigmoid(gate_act)
    grad_gate = (
        grad_active * up_proj * sigmoid_gate * (1.0 + gate_act * (1.0 - sigmoid_gate))
    ).astype(jnp.bfloat16)
    grad_up = (grad_active * gate_act * sigmoid_gate).astype(jnp.bfloat16)
    return (grad_gate, grad_up)


def slot_lanes(rows, slots):
    return lax.broadcasted_iota(jnp.int32, (rows, slots * ADAPTER_RANK), 1) // ADAPTER_RANK


def keep_slot(values, own_slot, parts=1):
    lanes = slot_lanes(values.shape[0], parts * ADAPTER_COUNT) % ADAPTER_COUNT
    return jnp.where(lanes == own_slot, values, 0.0).astype(jnp.bfloat16)


def take_slot(stacked, own_slot, parts):
    shaped = stacked.reshape(parts, ADAPTER_COUNT, ADAPTER_RANK, stacked.shape[-1])
    own = lax.dynamic_index_in_dim(shaped, own_slot, 1, keepdims=False)
    return own.reshape(parts * ADAPTER_RANK, stacked.shape[-1])


class Ring:
    def __init__(self, devices):
        self.chips = devices // 2
        order = list(range(0, self.chips, 2)) + list(range(1, self.chips, 2))[::-1]
        self.order = order
        ahead, behind = [], []
        for place, chip in enumerate(order):
            follower = order[(place + 1) % self.chips]
            for core in range(2):
                ahead.append((2 * chip + core, 2 * follower + core))
                behind.append((2 * follower + core, 2 * chip + core))
        self.ahead, self.behind = ahead, behind
        self.partner = [(i, i ^ 1) for i in range(devices)]
        self.far = self.chips // 2
        self.offsets = [0]
        for step in range(1, self.far):
            self.offsets += [-step, step]
        self.offsets.append(self.far)

    def forth(self, values):
        return lax.ppermute(values, "fsdp", self.ahead)

    def back(self, values):
        return lax.ppermute(values, "fsdp", self.behind)

    def swap(self, values):
        return lax.ppermute(values, "fsdp", self.partner)

    def source(self, offset, position):
        table = jnp.asarray(self.order, jnp.int32)
        return table[(position + offset) % self.chips]

    def gather(self, own):
        half = own.shape[0] // 2
        upper, lower = own[:half], own[half:]
        forth_up, forth_low, back_up, back_low = upper, lower, upper, lower
        chunks = {0: own}
        for step in range(1, self.far + 1):
            forth_up = self.forth(forth_up)
            back_low = self.back(back_low)
            if step < self.far:
                forth_low = self.forth(forth_low)
                back_up = self.back(back_up)
                chunks[-step] = jnp.concatenate([forth_up, forth_low], axis=0)
                chunks[step] = jnp.concatenate([back_up, back_low], axis=0)
            else:
                chunks[step] = jnp.concatenate([forth_up, back_low], axis=0)
        return chunks

    def scatter(self, partial):
        first = partial(self.far)
        half = first.shape[0] // 2
        low = lambda v: v.astype(jnp.bfloat16)
        forth_up = self.forth(low(first[:half]))
        back_low = self.back(low(first[half:]))
        forth_low = back_up = None
        for step in range(self.far - 1, 0, -1):
            ahead, behind = partial(step), partial(-step)
            forth_up = self.forth(low(forth_up.astype(jnp.float32) + ahead[:half]))
            back_low = self.back(low(back_low.astype(jnp.float32) + behind[half:]))
            later = ahead[half:] if forth_low is None else forth_low.astype(jnp.float32) + ahead[half:]
            forth_low = self.forth(low(later))
            later = behind[:half] if back_up is None else back_up.astype(jnp.float32) + behind[:half]
            back_up = self.back(low(later))
        own = partial(0)
        up = own[:half] + forth_up.astype(jnp.float32)
        down = own[half:] + back_low.astype(jnp.float32)
        if forth_low is not None:
            up = up + back_up.astype(jnp.float32)
            down = down + forth_low.astype(jnp.float32)
        return jnp.concatenate([up, down], axis=0)


def factor_columns(factor, parts):
    adapters, rows = factor.shape[:2]
    shaped = factor.reshape(adapters, rows, parts, ADAPTER_RANK)
    return shaped.transpose(1, 2, 0, 3).reshape(rows, parts * adapters * ADAPTER_RANK)


def factor_rows(factor):
    return factor.reshape(-1, factor.shape[-1]).T


def shards(
    group_size,
    replicas,
    residual_input,
    document_index,
    adapter_index,
    attention_gain,
    feedforward_gain,
    query_weight,
    key_weight,
    value_weight,
    output_weight,
    gate_weight,
    up_weight,
    down_weight,
    attention_input_factor,
    output_input_factor,
    feedforward_input_factor,
    down_input_factor,
    query_output_factor,
    key_output_factor,
    value_output_factor,
    output_output_factor,
    gate_output_factor,
    up_output_factor,
    down_output_factor,
    cotangent,
):
    low = lambda v: v.astype(jnp.bfloat16)
    ring = Ring(group_size)
    seq_len, width = residual_input.shape
    slots = ADAPTER_COUNT * ADAPTER_RANK
    own_slot = adapter_index[0]
    here = lax.axis_index("fsdp")
    core = here % 2
    place_of = [0] * ring.chips
    for place, chip in enumerate(ring.order):
        place_of[chip] = place
    position = jnp.asarray(place_of, jnp.int32)[here // 2]
    all_slots = lax.all_gather(adapter_index, "fsdp", axis=0, tiled=True)
    attn_gain_row = attention_gain[0].astype(jnp.float32)
    mlp_gain_row = feedforward_gain[0].astype(jnp.float32)

    key_part = query_weight.shape[1]
    kv_lift = jnp.concatenate(
        [factor_rows(key_output_factor[0]), factor_rows(value_output_factor[0])], axis=0
    )
    kv_width = kv_lift.size // key_part
    pieces = [
        query_weight[0],
        key_weight[0],
        value_weight[0],
        factor_columns(attention_input_factor[0], 3),
        output_weight[0],
        factor_columns(output_input_factor[0], 1),
        factor_columns(feedforward_input_factor[0], 2),
        factor_rows(query_output_factor[0]),
        factor_rows(output_output_factor[0]),
        factor_rows(down_output_factor[0]),
        kv_lift.reshape(key_part, kv_width),
    ]
    fetched = lax.all_gather(jnp.concatenate(pieces, axis=1), "fsdp", axis=0, tiled=True)
    q_width, kv_dim = query_weight.shape[2], key_weight.shape[2]
    ends = [0]
    for piece in pieces:
        ends.append(ends[-1] + piece.shape[1])
    in_w = fetched[:, : ends[4]]
    attn_in = fetched[:, ends[3] : ends[4]]
    out_w = fetched[:, ends[4] : ends[6]]
    mlp_in = fetched[:, ends[6] : ends[7]]
    lift_query = fetched[:, ends[7] : ends[8]]
    lift_out = fetched[:, ends[8] : ends[9]]
    lift_down = fetched[:, ends[9] : ends[10]]
    kv_all = fetched[:, ends[10] : ends[11]].reshape(group_size, 2, -1, slots)
    lift_key = kv_all[:, 0].reshape(kv_dim, slots)
    lift_value = kv_all[:, 1].reshape(kv_dim, slots)

    gate_pair = jnp.concatenate([gate_weight[0], ring.swap(gate_weight[0])], axis=1)
    up_pair = jnp.concatenate([up_weight[0], ring.swap(up_weight[0])], axis=1)
    both_w = jnp.concatenate([gate_pair, up_pair], axis=1)
    inner = gate_pair.shape[1]
    own_inner = inner // 2
    small_own = jnp.concatenate(
        [
            gate_output_factor[0].reshape(slots, own_inner),
            up_output_factor[0].reshape(slots, own_inner),
            factor_columns(down_input_factor[0], 1).T,
        ],
        axis=0,
    )
    small_both = jnp.concatenate([small_own, ring.swap(small_own)], axis=1)
    lift_gate, lift_up = small_both[:slots], small_both[slots : 2 * slots]
    down_in = small_both[2 * slots :].T
    nothing = jnp.zeros_like(lift_gate)
    lift_both = jnp.concatenate(
        [
            jnp.concatenate([lift_gate, nothing], axis=1),
            jnp.concatenate([nothing, lift_up], axis=1),
        ],
        axis=0,
    )
    lift_up_next = jnp.roll(lift_up, ADAPTER_RANK, axis=0)
    down_pair = jnp.concatenate([down_weight[0], ring.swap(down_weight[0])], axis=0)
    down_ext = jnp.concatenate([down_pair, down_in], axis=1)

    grad_top = cotangent.astype(jnp.float32)
    grad_mlp_own = low(resid_mult * grad_top)
    grad_chunks = ring.gather(grad_mlp_own)

    stream = residual_input.astype(jnp.float32)
    segment_row = document_index[0]
    positions = jnp.arange(seq_len, dtype=jnp.int32)
    allowed = (
        (segment_row[:, None] == segment_row[None, :]) & (positions[None, :] <= positions[:, None])
    )[None, None]
    cosine, sine_table = rope_tables(seq_len, HEAD_DIM)
    normed, inv_attn = norm_forward(stream, attn_gain_row)
    raw = plain_dot(normed, in_w)
    small_attn = keep_slot(raw[:, ends[3] :], own_slot, 3)
    query_raw = raw[:, :q_width] + outer_dot(small_attn[:, :slots], lift_query)
    key_raw = raw[:, ends[1] : ends[2]] + outer_dot(small_attn[:, slots : 2 * slots], lift_key)
    value_raw = raw[:, ends[2] : ends[3]] + outer_dot(small_attn[:, 2 * slots :], lift_value)
    queries = low(rotate(query_raw.reshape(seq_len, HEADS, HEAD_DIM), cosine, sine_table))
    key_rot = low(rotate(key_raw.reshape(seq_len, KV_HEADS, HEAD_DIM), cosine, sine_table))
    values = low(value_raw.reshape(seq_len, KV_HEADS, HEAD_DIM))
    grouped = queries.reshape(seq_len, KV_HEADS, HEADS // KV_HEADS, HEAD_DIM)
    scores = masked_scores(grouped, key_rot, allowed)
    row_top = jnp.max(scores, axis=-1, keepdims=True)
    exp_scores = jnp.exp(scores - row_top)
    total_sum = jnp.sum(exp_scores, axis=-1, keepdims=True)
    log_total = row_top + jnp.log(total_sum)
    probs_low = low(exp_scores / total_sum)
    mixed = jnp.einsum("khst,tke->skhe", probs_low, values, preferred_element_type=jnp.float32)
    mixed = low(mixed.reshape(seq_len, q_width))
    branch_ext = plain_dot(mixed, out_w)
    small_out = keep_slot(branch_ext[:, width:], own_slot)
    after_attn = stream + resid_mult * (branch_ext[:, :width] + outer_dot(small_out, lift_out))

    normed_mlp, inv_mlp = norm_forward(after_attn, mlp_gain_row)
    chunks = ring.gather(normed_mlp)
    batches = [[0]] + [[-step, step] for step in range(1, ring.far)] + [[ring.far]]
    kept = {}
    columns = {"active": [], "gate": [], "up": [], "small": [], "grad_small": []}
    for batch in batches:
        rows = jnp.concatenate([chunks[offset] for offset in batch], axis=0)
        grad_rows = jnp.concatenate([grad_chunks[offset] for offset in batch], axis=0)
        row_slot = jnp.concatenate(
            [
                jnp.full(
                    (seq_len, 1),
                    all_slots[2 * ring.source(offset, position) + core],
                    jnp.int32,
                )
                for offset in batch
            ],
            axis=0,
        )
        grad_small_down = keep_slot(plain_dot(grad_rows, lift_down), row_slot)
        grad_active = outer_dot(grad_rows, down_pair) + outer_dot(grad_small_down, down_in)
        small_mlp = keep_slot(plain_dot(rows, mlp_in), row_slot, 2)
        both = plain_dot(rows, both_w) + plain_dot(small_mlp, lift_both)
        gate_act, up_proj = both[:, :inner], both[:, inner:]
        active = low(gate_act * jax.nn.sigmoid(gate_act) * up_proj)
        grad_gate, grad_up = gate_grads(grad_active, gate_act, up_proj)
        lanes = slot_lanes(rows.shape[0], ADAPTER_COUNT)
        small_back = jnp.where(lanes == row_slot, outer_dot(grad_gate, lift_gate), 0.0) + jnp.where(
            lanes == (row_slot + 1) % ADAPTER_COUNT, outer_dot(grad_up, lift_up_next), 0.0
        )
        grad_both = jnp.concatenate([grad_gate, grad_up], axis=1)
        back = outer_dot(grad_both, both_w)
        forward = plain_dot(active, down_ext)
        for index, offset in enumerate(batch):
            span = slice(index * seq_len, (index + 1) * seq_len)
            kept[offset] = (
                jnp.concatenate([back[span], small_back[span]], axis=1),
                forward[span],
            )
        columns["active"].append(active)
        columns["gate"].append(grad_gate)
        columns["up"].append(grad_up)
        columns["small"].append(small_mlp)
        columns["grad_small"].append(grad_small_down)
    summed = ring.scatter(lambda offset: kept[offset][0])
    joined = {name: jnp.concatenate(parts, axis=0) for name, parts in columns.items()}
    grad_hidden = jnp.stack(
        [
            inner_dot(joined["grad_small"], joined["active"]),
            inner_dot(joined["small"][:, :slots], joined["gate"]),
            inner_dot(joined["small"][:, slots:], joined["up"]),
        ]
    )
    grad_hidden = grad_hidden[:, :, :own_inner] + ring.swap(grad_hidden[:, :, own_inner:])

    lanes = slot_lanes(seq_len, ADAPTER_COUNT)
    small_sum = summed[:, width:]
    grad_small_gate = low(jnp.where(lanes == own_slot, small_sum, 0.0))
    next_slot = (own_slot + 1) % ADAPTER_COUNT
    grad_small_up = jnp.roll(
        low(jnp.where(lanes == next_slot, small_sum, 0.0)), -ADAPTER_RANK, axis=1
    )
    grad_small_mlp = jnp.concatenate([grad_small_gate, grad_small_up], axis=1)
    grad_normed_mlp = summed[:, :width] + outer_dot(grad_small_mlp, mlp_in)
    grad_after = grad_top + norm_backward(grad_normed_mlp, after_attn, inv_mlp, mlp_gain_row)

    grad_attn = low(resid_mult * grad_after)
    grad_small_out = keep_slot(plain_dot(grad_attn, lift_out), own_slot)
    grad_mixed = low(
        outer_dot(grad_attn, out_w[:, :width]) + outer_dot(grad_small_out, out_w[:, width:])
    )
    grad_heads = grad_mixed.reshape(seq_len, KV_HEADS, HEADS // KV_HEADS, HEAD_DIM)
    probs_full = jnp.exp(masked_scores(grouped, key_rot, allowed) - log_total)
    probs_back = low(probs_full)
    grad_probs = jnp.einsum(
        "skhe,tke->khst", grad_heads, values, preferred_element_type=jnp.float32
    )
    delta_row = jnp.sum(probs_full * grad_probs, axis=-1, keepdims=True)
    grad_scores = low(probs_full * (grad_probs - delta_row))
    grad_queries = (
        jnp.einsum("khst,tke->skhe", grad_scores, key_rot, preferred_element_type=jnp.float32)
        * attn_mult
    )
    grad_keys = (
        jnp.einsum("khst,skhe->tke", grad_scores, grouped, preferred_element_type=jnp.float32)
        * attn_mult
    )
    grad_values = jnp.einsum(
        "khst,skhe->tke", probs_back, grad_heads, preferred_element_type=jnp.float32
    )
    grad_query_raw = rotate_back(grad_queries.reshape(seq_len, HEADS, HEAD_DIM), cosine, sine_table)
    grad_query_raw = low(grad_query_raw.reshape(seq_len, q_width))
    grad_key_raw = low(rotate_back(grad_keys, cosine, sine_table).reshape(seq_len, kv_dim))
    grad_value_raw = low(grad_values.reshape(seq_len, kv_dim))
    grad_small_attn = keep_slot(
        jnp.concatenate(
            [
                plain_dot(grad_query_raw, lift_query),
                plain_dot(grad_key_raw, lift_key),
                plain_dot(grad_value_raw, lift_value),
            ],
            axis=1,
        ),
        own_slot,
        3,
    )
    grad_raw = jnp.concatenate(
        [grad_query_raw, grad_key_raw, grad_value_raw, grad_small_attn], axis=1
    )
    grad_normed = outer_dot(grad_raw, in_w)
    grad_stream = grad_after + norm_backward(grad_normed, stream, inv_attn, attn_gain_row)

    forward_sum = ring.scatter(lambda offset: kept[offset][1])
    small_down = keep_slot(forward_sum[:, width:], own_slot)
    hidden_out = low(
        after_attn + resid_mult * (forward_sum[:, :width] + outer_dot(small_down, lift_down))
    )

    wide = jnp.concatenate(
        [
            take_slot(inner_dot(grad_small_attn, normed), own_slot, 3),
            take_slot(inner_dot(grad_small_out, mixed), own_slot, 1),
            take_slot(inner_dot(grad_small_mlp, normed_mlp), own_slot, 2),
            take_slot(inner_dot(small_attn[:, :slots], grad_query_raw), own_slot, 1),
            take_slot(inner_dot(small_out, grad_attn), own_slot, 1),
            take_slot(inner_dot(small_down, grad_mlp_own), own_slot, 1),
        ],
        axis=0,
    )
    narrow = jnp.concatenate(
        [
            take_slot(inner_dot(small_attn[:, slots : 2 * slots], grad_key_raw), own_slot, 1),
            take_slot(inner_dot(small_attn[:, 2 * slots :], grad_value_raw), own_slot, 1),
        ],
        axis=0,
    )
    wide_rows, share = wide.shape[0], width // group_size
    narrow_share = kv_dim // group_size
    wide = low(wide).reshape(wide_rows, group_size, share).transpose(1, 0, 2)
    narrow = low(narrow).reshape(2 * ADAPTER_RANK, group_size, narrow_share).transpose(1, 0, 2)
    narrow = narrow.reshape(group_size, -1, share)
    parcel = jnp.concatenate([wide, narrow], axis=1)
    parcel = lax.all_to_all(parcel, "fsdp", 0, 0, tiled=True)
    chosen = all_slots[:, None] == jnp.arange(ADAPTER_COUNT, dtype=jnp.int32)[None, :]
    owned = jnp.sum(
        jnp.where(chosen[:, :, None, None], parcel[:, None].astype(jnp.float32), 0.0), axis=0
    )
    owned = low(owned)
    grad_hidden = low(grad_hidden)
    if replicas == 2:
        other = [(0, 1), (1, 0)]
        owned = owned.astype(jnp.float32) + lax.ppermute(owned, "rep", other).astype(jnp.float32)
        grad_hidden = grad_hidden.astype(jnp.float32) + lax.ppermute(
            grad_hidden, "rep", other
        ).astype(jnp.float32)
    else:
        owned = lax.psum(owned, "rep").astype(jnp.float32)
        grad_hidden = lax.psum(grad_hidden, "rep").astype(jnp.float32)

    rank = ADAPTER_RANK
    rows_of = lambda first, count: owned[:, first * rank : (first + count) * rank]
    turned = lambda v: v.transpose(0, 2, 1)[None]
    narrow = owned[:, wide_rows:].reshape(ADAPTER_COUNT, 2, rank, narrow_share)
    hidden = grad_hidden.reshape(3, ADAPTER_COUNT, rank, own_inner)
    return (
        hidden_out,
        grad_stream,
        turned(rows_of(0, 3)),
        turned(rows_of(3, 1)),
        turned(rows_of(4, 2)),
        turned(hidden[0]),
        rows_of(6, 1)[None],
        narrow[:, 0][None],
        narrow[:, 1][None],
        rows_of(7, 1)[None],
        hidden[1][None],
        hidden[2][None],
        rows_of(8, 1)[None],
    )


def solution(mesh):
    return jax.shard_map(
        partial(shards, mesh.shape["fsdp"], mesh.shape["rep"]),
        mesh=mesh,
        in_specs=(
            P(("rep", "fsdp"), None),
            P(("rep", "fsdp"), None),
            P(("rep", "fsdp")),
            P(),
            P(),
            P(None, "fsdp", None),
            P(None, "fsdp", None),
            P(None, "fsdp", None),
            P(None, "fsdp", None),
            P(None, None, "fsdp"),
            P(None, None, "fsdp"),
            P(None, "fsdp", None),
            P(None, None, "fsdp", None),
            P(None, None, "fsdp", None),
            P(None, None, "fsdp", None),
            P(None, None, "fsdp", None),
            P(None, None, None, "fsdp"),
            P(None, None, None, "fsdp"),
            P(None, None, None, "fsdp"),
            P(None, None, None, "fsdp"),
            P(None, None, None, "fsdp"),
            P(None, None, None, "fsdp"),
            P(None, None, None, "fsdp"),
            P(("rep", "fsdp"), None),
        ),
        out_specs=(
            P(("rep", "fsdp"), None),
            P(("rep", "fsdp"), None),
            P(None, None, "fsdp", None),
            P(None, None, "fsdp", None),
            P(None, None, "fsdp", None),
            P(None, None, "fsdp", None),
            P(None, None, None, "fsdp"),
            P(None, None, None, "fsdp"),
            P(None, None, None, "fsdp"),
            P(None, None, None, "fsdp"),
            P(None, None, None, "fsdp"),
            P(None, None, None, "fsdp"),
            P(None, None, None, "fsdp"),
        ),
        check_vma=False,
    )
```

```python
from functools import partial

import jax
import jax.numpy as jnp
from jax import lax
from jax.experimental import pallas as pl
from jax.experimental.pallas import tpu as pltpu
from jax.sharding import PartitionSpec as P

HEADS = 32
KV_HEADS = 8
HEAD_DIM = 64
ADAPTER_RANK = 16
ADAPTER_COUNT = 8


eps = 1e-05
attn_mult = 0.015625
resid_mult = 0.22
rope_base = 10000000.0
neg_big = -1e30


def plain_dot(left_op, right_op):
    return jnp.dot(left_op, right_op, preferred_element_type=jnp.float32)


def inner_dot(left_op, right_op):
    return lax.dot_general(
        left_op, right_op, (((0,), (0,)), ((), ())), preferred_element_type=jnp.float32
    )


def outer_dot(left_op, right_op):
    return lax.dot_general(
        left_op, right_op, (((1,), (1,)), ((), ())), preferred_element_type=jnp.float32
    )


def norm_forward(stream, gain_row):
    inv_scale = lax.rsqrt(jnp.mean(stream * stream, axis=-1, keepdims=True) + eps)
    return ((stream * inv_scale * gain_row).astype(jnp.bfloat16), inv_scale)


def norm_backward(grad_normed, stream, inv_scale, gain_row):
    weighted = grad_normed * gain_row
    return inv_scale * weighted - stream * inv_scale**3 * jnp.mean(
        weighted * stream, axis=-1, keepdims=True
    )


def rope_tables(seq_len, head_dim):
    half_dim = head_dim // 2
    frequency = rope_base ** (-2.0 * jnp.arange(half_dim, dtype=jnp.float32) / head_dim)
    angles = jnp.arange(seq_len, dtype=jnp.float32)[:, None] * frequency[None, :]
    return (jnp.cos(angles)[:, None, :], jnp.sin(angles)[:, None, :])


def rotate(vector, cosine, sine_table):
    half_dim = vector.shape[-1] // 2
    former = vector[..., :half_dim]
    latter = vector[..., half_dim:]
    return jnp.concatenate(
        [former * cosine - latter * sine_table, latter * cosine + former * sine_table], axis=-1
    )


def rotate_back(vector, cosine, sine_table):
    half_dim = vector.shape[-1] // 2
    former = vector[..., :half_dim]
    latter = vector[..., half_dim:]
    return jnp.concatenate(
        [former * cosine + latter * sine_table, latter * cosine - former * sine_table], axis=-1
    )


def masked_scores(grouped, key_rot, allowed):
    scores = (
        jnp.einsum("skhe,tke->khst", grouped, key_rot, preferred_element_type=jnp.float32)
        * attn_mult
    )
    return jnp.where(allowed, scores, neg_big)


def gate_grads(grad_active, gate_act, up_proj):
    sigmoid_gate = jax.nn.sigmoid(gate_act)
    grad_gate = (
        grad_active * up_proj * sigmoid_gate * (1.0 + gate_act * (1.0 - sigmoid_gate))
    ).astype(jnp.bfloat16)
    grad_up = (grad_active * gate_act * sigmoid_gate).astype(jnp.bfloat16)
    return (grad_gate, grad_up)


def slot_lanes(rows, slots):
    return lax.broadcasted_iota(jnp.int32, (rows, slots * ADAPTER_RANK), 1) // ADAPTER_RANK


def keep_slot(values, own_slot, parts=1):
    lanes = slot_lanes(values.shape[0], parts * ADAPTER_COUNT) % ADAPTER_COUNT
    return jnp.where(lanes == own_slot, values, 0.0).astype(jnp.bfloat16)


def take_slot(stacked, own_slot, parts):
    shaped = stacked.reshape(parts, ADAPTER_COUNT, ADAPTER_RANK, stacked.shape[-1])
    own = lax.dynamic_index_in_dim(shaped, own_slot, 1, keepdims=False)
    return own.reshape(parts * ADAPTER_RANK, stacked.shape[-1])


class Ring:
    def __init__(self, devices):
        self.chips = devices // 2
        order = list(range(0, self.chips, 2)) + list(range(1, self.chips, 2))[::-1]
        self.order = order
        ahead, behind = [], []
        for place, chip in enumerate(order):
            follower = order[(place + 1) % self.chips]
            for core in range(2):
                ahead.append((2 * chip + core, 2 * follower + core))
                behind.append((2 * follower + core, 2 * chip + core))
        self.ahead, self.behind = ahead, behind
        self.partner = [(i, i ^ 1) for i in range(devices)]
        self.lanes = [list(range(core, devices, 2)) for core in range(2)]
        self.far = self.chips // 2
        self.offsets = [0]
        for step in range(1, self.far):
            self.offsets += [-step, step]
        self.offsets.append(self.far)

    def forth(self, values):
        return lax.ppermute(values, "fsdp", self.ahead)

    def back(self, values):
        return lax.ppermute(values, "fsdp", self.behind)

    def swap(self, values):
        return lax.ppermute(values, "fsdp", self.partner)

    def source(self, offset, position):
        table = jnp.asarray(self.order, jnp.int32)
        return table[(position + offset) % self.chips]

    def gather(self, own):
        return Gather(self, own)

    def scatter(self, partial, gates=()):
        gates = dict(zip(range(self.far, -1, -1), gates))
        wide = lambda v: v.astype(jnp.float32)
        held = lambda v, step: after(v, gates[step]) if step in gates else v
        add = lambda v, share: (wide(v) + wide(share)).astype(jnp.bfloat16)
        upper, lower = held(partial[self.far], self.far)
        forth_up, back_low = self.forth(upper), self.back(lower)
        forth_low = back_up = None
        for step in range(self.far - 1, 0, -1):
            ahead, behind = held((partial[step], partial[-step]), step)
            forth_low = self.forth(ahead[1] if forth_low is None else add(forth_low, ahead[1]))
            back_up = self.back(behind[0] if back_up is None else add(back_up, behind[0]))
            forth_up = self.forth(add(forth_up, ahead[0]))
            back_low = self.back(add(back_low, behind[1]))
        own = held(partial[0], 0)
        up = wide(own[0]) + wide(forth_up)
        down = wide(own[1]) + wide(back_low)
        if forth_low is not None:
            up = up + wide(back_up)
            down = down + wide(forth_low)
        return jnp.concatenate([up, down], axis=0)


class Gather:
    def __init__(self, ring, own):
        self.ring, self.done = ring, 0
        half = own.shape[0] // 2
        self.forth_up = self.back_up = own[:half]
        self.forth_low = self.back_low = own[half:]
        self.chunks = {0: (own[:half], own[half:])}

    def step(self, gate=None):
        ring = self.ring
        self.done += 1
        held = (lambda v: v) if gate is None else (lambda v: after(v, gate))
        last = self.done == ring.far
        self.forth_up = ring.forth(held(self.forth_up))
        self.back_low = ring.back(held(self.back_low))
        if last:
            self.chunks[self.done] = (self.forth_up, self.back_low)
            return
        self.forth_low = ring.forth(held(self.forth_low))
        self.back_up = ring.back(held(self.back_up))
        self.chunks[-self.done] = (self.forth_up, self.forth_low)
        self.chunks[self.done] = (self.back_up, self.back_low)


def after(values, earlier):
    return lax.optimization_barrier((values, earlier))[0]


def hidden_body(count, half, slot_ref, *refs):
    pieces = 2 * count
    rows_in, grads_in = refs[:pieces], refs[pieces : 2 * pieces]
    mlp_in, lift_down, gate_w, up_w, down_ext, lift_gate, lift_up, sums_in = refs[2 * pieces : 2 * pieces + 8]
    refs = refs[2 * pieces + 8 :]
    backs, aheads, sums = refs[:pieces], refs[pieces : 2 * pieces], refs[2 * pieces]
    rows, grads, small, grad_small, back, back_small, ahead = refs[2 * pieces + 1 :]
    tile = pl.program_id(0)
    width = rows.shape[1]
    slots = lift_gate.shape[0]
    low = lambda v: v.astype(jnp.bfloat16)

    def own_columns(values, index):
        lanes = lax.broadcasted_iota(jnp.int32, values.shape, 1) % slots // ADAPTER_RANK
        return jnp.where(lanes == slot_ref[index], values, 0.0)

    spans = [slice(2 * half * index, 2 * half * (index + 1)) for index in range(count)]

    @pl.when(tile == 0)
    def _():
        for index in range(pieces):
            rows[index * half : (index + 1) * half, :] = rows_in[index][...]
            grads[index * half : (index + 1) * half, :] = grads_in[index][...]
        small_all = plain_dot(rows[...], mlp_in[...])
        grad_all = plain_dot(grads[...], lift_down[...])
        for index, span in enumerate(spans):
            small[span, :] = low(own_columns(small_all[span], index))
            grad_small[span, :] = low(own_columns(grad_all[span], index))

    gate_act = plain_dot(rows[...], gate_w[...]) + plain_dot(small[:, :slots], lift_gate[...])
    up_proj = plain_dot(rows[...], up_w[...]) + plain_dot(small[:, slots:], lift_up[...])
    grad_active = outer_dot(grads[...], down_ext[:, :width]) + outer_dot(grad_small[...], down_ext[:, width:])
    sigmoid_gate = jax.nn.sigmoid(gate_act)
    active = low(gate_act * sigmoid_gate * up_proj)
    grad_gate = low(grad_active * up_proj * sigmoid_gate * (1.0 + gate_act * (1.0 - sigmoid_gate)))
    grad_up = low(grad_active * gate_act * sigmoid_gate)
    sums[0] = sums_in[0] + inner_dot(grad_small[...], active)
    sums[1] = sums_in[1] + inner_dot(small[:, :slots], grad_gate)
    sums[2] = sums_in[2] + inner_dot(small[:, slots:], grad_up)
    more_back = outer_dot(grad_gate, gate_w[...]) + outer_dot(grad_up, up_w[...])
    more_gate, more_up = outer_dot(grad_gate, lift_gate[...]), outer_dot(grad_up, lift_up[...])
    more_ahead = plain_dot(active, down_ext[...])

    @pl.when(tile == 0)
    def _():
        back[...] = more_back
        back_small[:, :slots] = more_gate
        back_small[:, slots:] = more_up
        ahead[...] = more_ahead

    @pl.when(tile > 0)
    def _():
        back[...] += more_back
        back_small[:, :slots] += more_gate
        back_small[:, slots:] += more_up
        ahead[...] += more_ahead

    @pl.when(tile == pl.num_programs(0) - 1)
    def _():
        for index in range(count):
            both = own_columns(back_small[spans[index], :], index)
            joined = low(both[:, :slots] + pltpu.roll(both[:, slots:], ADAPTER_RANK, axis=1))
            for part in range(2):
                place = 2 * index + part
                own = slice(place * half, (place + 1) * half)
                backs[place][:, :width] = low(back[own, :])
                backs[place][:, width:] = joined[part * half : (part + 1) * half]
                aheads[place][...] = low(ahead[own, :])


def hidden_units(slot, rows, grads, weights, sums):
    mlp_in, lift_down, gate_w, up_w, down_ext, lift_gate, lift_up = weights
    count, pieces = len(rows) // 2, len(rows)
    half, width = rows[0].shape
    slots, inner = lift_gate.shape
    wide = down_ext.shape[1]
    tile = min(256, inner)
    total = pieces * half
    whole = lambda shape: pl.BlockSpec(shape, lambda h, *_: (0,) * len(shape), pipeline_mode=pl.Buffered(1))
    across = lambda first: pl.BlockSpec((first, tile), lambda h, *_: (0, h))
    sums_spec = pl.BlockSpec((3, slots, tile), lambda h, *_: (0, 0, h))
    spec = pltpu.PrefetchScalarGridSpec(
        num_scalar_prefetch=1,
        grid=(inner // tile,),
        in_specs=[whole((half, width))] * (2 * pieces)
        + [
            whole(mlp_in.shape),
            whole(lift_down.shape),
            across(width),
            across(width),
            pl.BlockSpec((tile, wide), lambda h, *_: (h, 0)),
            across(slots),
            across(slots),
            sums_spec,
        ],
        out_specs=[whole((half, wide))] * (2 * pieces) + [sums_spec],
        scratch_shapes=[
            pltpu.VMEM((total, width), jnp.bfloat16),
            pltpu.VMEM((total, width), jnp.bfloat16),
            pltpu.VMEM((total, 2 * slots), jnp.bfloat16),
            pltpu.VMEM((total, slots), jnp.bfloat16),
            pltpu.VMEM((total, width), jnp.float32),
            pltpu.VMEM((total, 2 * slots), jnp.float32),
            pltpu.VMEM((total, wide), jnp.float32),
        ],
    )
    results = pl.pallas_call(
        partial(hidden_body, count, half),
        out_shape=[jax.ShapeDtypeStruct((half, wide), jnp.bfloat16)] * (2 * pieces)
        + [jax.ShapeDtypeStruct(sums.shape, jnp.float32)],
        grid_spec=spec,
        input_output_aliases={2 * pieces + 8: 2 * pieces},
        cost_estimate=pl.CostEstimate(
            flops=2 * total * inner * 6 * width,
            transcendentals=total * inner,
            bytes_accessed=6 * width * inner + 8 * total * width,
        ),
        name="hidden_units",
    )(slot, *rows, *grads, *weights, sums)
    return results[:pieces], results[pieces : 2 * pieces], results[-1]


def factor_columns(factor, parts):
    adapters, rows = factor.shape[:2]
    shaped = factor.reshape(adapters, rows, parts, ADAPTER_RANK)
    return shaped.transpose(1, 2, 0, 3).reshape(rows, parts * adapters * ADAPTER_RANK)


def factor_rows(factor):
    return factor.reshape(-1, factor.shape[-1]).T


def shards(
    group_size,
    replicas,
    residual_input,
    document_index,
    adapter_index,
    attention_gain,
    feedforward_gain,
    query_weight,
    key_weight,
    value_weight,
    output_weight,
    gate_weight,
    up_weight,
    down_weight,
    attention_input_factor,
    output_input_factor,
    feedforward_input_factor,
    down_input_factor,
    query_output_factor,
    key_output_factor,
    value_output_factor,
    output_output_factor,
    gate_output_factor,
    up_output_factor,
    down_output_factor,
    cotangent,
):
    low = lambda v: v.astype(jnp.bfloat16)
    ring = Ring(group_size)
    seq_len, width = residual_input.shape
    slots = ADAPTER_COUNT * ADAPTER_RANK
    own_slot = adapter_index[0]
    here = lax.axis_index("fsdp")
    core = here % 2
    place_of = [0] * ring.chips
    for place, chip in enumerate(ring.order):
        place_of[chip] = place
    position = jnp.asarray(place_of, jnp.int32)[here // 2]
    attn_gain_row = attention_gain[0].astype(jnp.float32)
    mlp_gain_row = feedforward_gain[0].astype(jnp.float32)

    key_part = query_weight.shape[1]
    kv_lift = jnp.concatenate(
        [factor_rows(key_output_factor[0]), factor_rows(value_output_factor[0])], axis=0
    )
    kv_width = kv_lift.size // key_part
    pieces = [
        query_weight[0],
        key_weight[0],
        value_weight[0],
        factor_columns(attention_input_factor[0], 3),
        output_weight[0],
        factor_columns(output_input_factor[0], 1),
        factor_columns(feedforward_input_factor[0], 2),
        factor_rows(query_output_factor[0]),
        factor_rows(output_output_factor[0]),
        factor_rows(down_output_factor[0]),
        kv_lift.reshape(key_part, kv_width),
        jnp.full((key_part, kv_width), own_slot, jnp.int32).astype(jnp.bfloat16),
    ]
    fetched = lax.all_gather(jnp.concatenate(pieces, axis=1), "fsdp", axis=0, tiled=True)
    q_width, kv_dim = query_weight.shape[2], key_weight.shape[2]
    ends = [0]
    for piece in pieces:
        ends.append(ends[-1] + piece.shape[1])
    in_w = fetched[:, : ends[4]]
    attn_in = fetched[:, ends[3] : ends[4]]
    out_w = fetched[:, ends[4] : ends[6]]
    mlp_in = fetched[:, ends[6] : ends[7]]
    lift_query = fetched[:, ends[7] : ends[8]]
    lift_out = fetched[:, ends[8] : ends[9]]
    lift_down = fetched[:, ends[9] : ends[10]]
    kv_all = fetched[:, ends[10] : ends[11]].reshape(group_size, 2, -1, slots)
    all_slots = fetched[::key_part, ends[11]].astype(jnp.int32)
    lift_key = kv_all[:, 0].reshape(kv_dim, slots)
    lift_value = kv_all[:, 1].reshape(kv_dim, slots)

    gate_pair = jnp.concatenate([gate_weight[0], ring.swap(gate_weight[0])], axis=1)
    up_pair = jnp.concatenate([up_weight[0], ring.swap(up_weight[0])], axis=1)
    inner = gate_pair.shape[1]
    own_inner = inner // 2
    small_own = jnp.concatenate(
        [
            gate_output_factor[0].reshape(slots, own_inner),
            up_output_factor[0].reshape(slots, own_inner),
            factor_columns(down_input_factor[0], 1).T,
        ],
        axis=0,
    )
    small_both = jnp.concatenate([small_own, ring.swap(small_own)], axis=1)
    lift_gate, lift_up = small_both[:slots], small_both[slots : 2 * slots]
    down_in = small_both[2 * slots :].T
    down_pair = jnp.concatenate([down_weight[0], ring.swap(down_weight[0])], axis=0)
    down_ext = jnp.concatenate([down_pair, down_in], axis=1)

    grad_top = cotangent.astype(jnp.float32)
    grad_mlp_own = low(resid_mult * grad_top)
    grad_ring = ring.gather(grad_mlp_own)

    stream = residual_input.astype(jnp.float32)
    segment_row = document_index[0]
    positions = jnp.arange(seq_len, dtype=jnp.int32)
    allowed = (
        (segment_row[:, None] == segment_row[None, :]) & (positions[None, :] <= positions[:, None])
    )[None, None]
    cosine, sine_table = rope_tables(seq_len, HEAD_DIM)
    normed, inv_attn = norm_forward(stream, attn_gain_row)
    grad_ring.step(fetched)
    raw = plain_dot(normed, in_w)
    small_attn = keep_slot(raw[:, ends[3] :], own_slot, 3)
    query_raw = raw[:, :q_width] + outer_dot(small_attn[:, :slots], lift_query)
    key_raw = raw[:, ends[1] : ends[2]] + outer_dot(small_attn[:, slots : 2 * slots], lift_key)
    value_raw = raw[:, ends[2] : ends[3]] + outer_dot(small_attn[:, 2 * slots :], lift_value)
    queries = low(rotate(query_raw.reshape(seq_len, HEADS, HEAD_DIM), cosine, sine_table))
    key_rot = low(rotate(key_raw.reshape(seq_len, KV_HEADS, HEAD_DIM), cosine, sine_table))
    values = low(value_raw.reshape(seq_len, KV_HEADS, HEAD_DIM))
    grouped = queries.reshape(seq_len, KV_HEADS, HEADS // KV_HEADS, HEAD_DIM)
    scores = masked_scores(grouped, key_rot, allowed)
    grad_ring.step(scores)
    row_top = jnp.max(scores, axis=-1, keepdims=True)
    exp_scores = jnp.exp(scores - row_top)
    total_sum = jnp.sum(exp_scores, axis=-1, keepdims=True)
    log_total = row_top + jnp.log(total_sum)
    probs_low = low(exp_scores / total_sum)
    mixed = jnp.einsum("khst,tke->skhe", probs_low, values, preferred_element_type=jnp.float32)
    mixed = low(mixed.reshape(seq_len, q_width))
    branch_ext = plain_dot(mixed, out_w)
    small_out = keep_slot(branch_ext[:, width:], own_slot)
    after_attn = stream + resid_mult * (branch_ext[:, :width] + outer_dot(small_out, lift_out))

    normed_mlp, inv_mlp = norm_forward(after_attn, mlp_gain_row)
    normed_ring = ring.gather(normed_mlp)
    normed_ring.step()
    for step in range(2, ring.far + 1):
        grad_ring.step(normed_ring.chunks[step - 1] if step > 2 else None)
        normed_ring.step()
    chunks, grad_chunks = normed_ring.chunks, grad_ring.chunks
    weights = (mlp_in, lift_down, gate_pair, up_pair, down_ext, lift_gate, lift_up)
    sums = jnp.zeros((3, slots, inner), jnp.float32)
    backs, aheads = {}, {}
    for step in range(ring.far + 1):
        batch = [-step, step] if 0 < step < ring.far else [step]
        slot = jnp.stack([all_slots[2 * ring.source(offset, position) + core] for offset in batch])
        rows = [piece for offset in batch for piece in chunks[offset]]
        grads = [piece for offset in batch for piece in grad_chunks[offset]]
        back, ahead, sums = hidden_units(slot, rows, grads, weights, sums)
        for index, offset in enumerate(batch):
            backs[offset] = tuple(back[2 * index : 2 * index + 2])
            aheads[offset] = tuple(ahead[2 * index : 2 * index + 2])
    grad_hidden = sums
    summed = ring.scatter(backs)
    grad_hidden = grad_hidden[:, :, :own_inner] + ring.swap(grad_hidden[:, :, own_inner:])

    lanes = slot_lanes(seq_len, ADAPTER_COUNT)
    small_sum = summed[:, width:]
    grad_small_gate = low(jnp.where(lanes == own_slot, small_sum, 0.0))
    next_slot = (own_slot + 1) % ADAPTER_COUNT
    grad_small_up = jnp.roll(
        low(jnp.where(lanes == next_slot, small_sum, 0.0)), -ADAPTER_RANK, axis=1
    )
    grad_small_mlp = jnp.concatenate([grad_small_gate, grad_small_up], axis=1)
    grad_normed_mlp = summed[:, :width] + outer_dot(grad_small_mlp, mlp_in)
    grad_after = grad_top + norm_backward(grad_normed_mlp, after_attn, inv_mlp, mlp_gain_row)

    grad_attn = low(resid_mult * grad_after)
    grad_small_out = keep_slot(plain_dot(grad_attn, lift_out), own_slot)
    grad_mixed = low(
        outer_dot(grad_attn, out_w[:, :width]) + outer_dot(grad_small_out, out_w[:, width:])
    )
    grad_heads = grad_mixed.reshape(seq_len, KV_HEADS, HEADS // KV_HEADS, HEAD_DIM)
    probs_full = jnp.exp(masked_scores(grouped, key_rot, allowed) - log_total)
    probs_back = low(probs_full)
    grad_probs = jnp.einsum(
        "skhe,tke->khst", grad_heads, values, preferred_element_type=jnp.float32
    )
    delta_row = jnp.sum(probs_full * grad_probs, axis=-1, keepdims=True)
    grad_scores = low(probs_full * (grad_probs - delta_row))
    grad_queries = (
        jnp.einsum("khst,tke->skhe", grad_scores, key_rot, preferred_element_type=jnp.float32)
        * attn_mult
    )
    grad_keys = (
        jnp.einsum("khst,skhe->tke", grad_scores, grouped, preferred_element_type=jnp.float32)
        * attn_mult
    )
    grad_values = jnp.einsum(
        "khst,skhe->tke", probs_back, grad_heads, preferred_element_type=jnp.float32
    )
    grad_query_raw = rotate_back(grad_queries.reshape(seq_len, HEADS, HEAD_DIM), cosine, sine_table)
    grad_query_raw = low(grad_query_raw.reshape(seq_len, q_width))
    grad_key_raw = low(rotate_back(grad_keys, cosine, sine_table).reshape(seq_len, kv_dim))
    grad_value_raw = low(grad_values.reshape(seq_len, kv_dim))
    grad_small_attn = keep_slot(
        jnp.concatenate(
            [
                plain_dot(grad_query_raw, lift_query),
                plain_dot(grad_key_raw, lift_key),
                plain_dot(grad_value_raw, lift_value),
            ],
            axis=1,
        ),
        own_slot,
        3,
    )
    grad_raw = jnp.concatenate(
        [grad_query_raw, grad_key_raw, grad_value_raw, grad_small_attn], axis=1
    )
    grad_normed = outer_dot(grad_raw, in_w)
    grad_stream = grad_after + norm_backward(grad_normed, stream, inv_attn, attn_gain_row)

    forward_sum = ring.scatter(
        aheads, (summed, grad_mixed, grad_scores, grad_raw)
    )
    small_down = keep_slot(forward_sum[:, width:], own_slot)
    hidden_out = low(
        after_attn + resid_mult * (forward_sum[:, :width] + outer_dot(small_down, lift_down))
    )

    wide = jnp.concatenate(
        [
            take_slot(inner_dot(grad_small_attn, normed), own_slot, 3),
            take_slot(inner_dot(grad_small_out, mixed), own_slot, 1),
            take_slot(inner_dot(grad_small_mlp, normed_mlp), own_slot, 2),
            take_slot(inner_dot(small_attn[:, :slots], grad_query_raw), own_slot, 1),
            take_slot(inner_dot(small_out, grad_attn), own_slot, 1),
            take_slot(inner_dot(small_down, grad_mlp_own), own_slot, 1),
        ],
        axis=0,
    )
    narrow = jnp.concatenate(
        [
            take_slot(inner_dot(small_attn[:, slots : 2 * slots], grad_key_raw), own_slot, 1),
            take_slot(inner_dot(small_attn[:, 2 * slots :], grad_value_raw), own_slot, 1),
        ],
        axis=0,
    )
    wide_rows, share = wide.shape[0], width // group_size
    narrow_share = kv_dim // group_size
    wide = low(wide).reshape(wide_rows, group_size, share).transpose(1, 0, 2)
    narrow = low(narrow).reshape(2 * ADAPTER_RANK, group_size, narrow_share).transpose(1, 0, 2)
    narrow = narrow.reshape(group_size, -1, share)
    parcel = jnp.concatenate([wide, narrow], axis=1)
    parcel = lax.all_to_all(parcel, "fsdp", 0, 0, tiled=True)
    chosen = all_slots[:, None] == jnp.arange(ADAPTER_COUNT, dtype=jnp.int32)[None, :]
    owned = jnp.sum(
        jnp.where(chosen[:, :, None, None], parcel[:, None].astype(jnp.float32), 0.0), axis=0
    )
    owned = low(owned)
    grad_hidden = low(grad_hidden)
    if replicas == 2:
        other = [(0, 1), (1, 0)]
        owned = owned.astype(jnp.float32) + lax.ppermute(owned, "rep", other).astype(jnp.float32)
        grad_hidden = grad_hidden.astype(jnp.float32) + lax.ppermute(
            grad_hidden, "rep", other
        ).astype(jnp.float32)
    else:
        owned = lax.psum(owned, "rep").astype(jnp.float32)
        grad_hidden = lax.psum(grad_hidden, "rep").astype(jnp.float32)

    rank = ADAPTER_RANK
    rows_of = lambda first, count: owned[:, first * rank : (first + count) * rank]
    turned = lambda v: v.transpose(0, 2, 1)[None]
    narrow = owned[:, wide_rows:].reshape(ADAPTER_COUNT, 2, rank, narrow_share)
    hidden = grad_hidden.reshape(3, ADAPTER_COUNT, rank, own_inner)
    return (
        hidden_out,
        grad_stream,
        turned(rows_of(0, 3)),
        turned(rows_of(3, 1)),
        turned(rows_of(4, 2)),
        turned(hidden[0]),
        rows_of(6, 1)[None],
        narrow[:, 0][None],
        narrow[:, 1][None],
        rows_of(7, 1)[None],
        hidden[1][None],
        hidden[2][None],
        rows_of(8, 1)[None],
    )


def solution(mesh):
    return jax.shard_map(
        partial(shards, mesh.shape["fsdp"], mesh.shape["rep"]),
        mesh=mesh,
        in_specs=(
            P(("rep", "fsdp"), None),
            P(("rep", "fsdp"), None),
            P(("rep", "fsdp")),
            P(),
            P(),
            P(None, "fsdp", None),
            P(None, "fsdp", None),
            P(None, "fsdp", None),
            P(None, "fsdp", None),
            P(None, None, "fsdp"),
            P(None, None, "fsdp"),
            P(None, "fsdp", None),
            P(None, None, "fsdp", None),
            P(None, None, "fsdp", None),
            P(None, None, "fsdp", None),
            P(None, None, "fsdp", None),
            P(None, None, None, "fsdp"),
            P(None, None, None, "fsdp"),
            P(None, None, None, "fsdp"),
            P(None, None, None, "fsdp"),
            P(None, None, None, "fsdp"),
            P(None, None, None, "fsdp"),
            P(None, None, None, "fsdp"),
            P(("rep", "fsdp"), None),
        ),
        out_specs=(
            P(("rep", "fsdp"), None),
            P(("rep", "fsdp"), None),
            P(None, None, "fsdp", None),
            P(None, None, "fsdp", None),
            P(None, None, "fsdp", None),
            P(None, None, "fsdp", None),
            P(None, None, None, "fsdp"),
            P(None, None, None, "fsdp"),
            P(None, None, None, "fsdp"),
            P(None, None, None, "fsdp"),
            P(None, None, None, "fsdp"),
            P(None, None, None, "fsdp"),
            P(None, None, None, "fsdp"),
        ),
        check_vma=False,
    )
```
